1024 devices in a mesh: pipe: 8 (over x, core), ctx: 8 (over z_lo), dp: 16 (over z_hi, y).
Axes of the slice: x: 4, y: 4, z: 32 (z_hi: 4, z_lo: 8; z = z_hi * 8 + z_lo), core: 2. Of those that a mesh axis runs over, the one named last changes fastest.
Arguments:
- section_held: bfloat16 [8, 16, 2048, 1024], P('pipe', 'dp', 'ctx'), may hold values from -6 to 6
- segments: int32 [8, 16, 2048], P('pipe', 'dp'), may hold values from 0 to 3, never falling along the last dimension, each value on 1 to 1024 neighbouring positions
- norm_gain: float32 [8, 1024], P('pipe'), may hold values from 0.1 to 1.9
- w_qkv: bfloat16 [8, 1024, 1536], P('pipe')
- w_out: bfloat16 [8, 512, 1024], P('pipe'), may hold values from -1 to 1
- grad_parts: float32 [8, 8, 16, 524288], P('pipe', 'ctx', 'dp'), may hold values from -2 to 2
- master: float32 [8, 524288], P('pipe', ('ctx', 'dp')), may hold values from -0.25 to 0.25
- moment: float32 [8, 524288], P('pipe', ('ctx', 'dp')), may hold values from -4 to 4
- second: float32 [8, 524288], P('pipe', ('ctx', 'dp')), may hold values from 0.1 to 1
Outputs:
- section_next: bfloat16 [8, 16, 2048, 1024], P('pipe', 'dp', 'ctx')
- new_master: float32 [8, 524288], P('pipe', ('ctx', 'dp'))
- new_moment: float32 [8, 524288], P('pipe', ('ctx', 'dp'))
- new_second: float32 [8, 524288], P('pipe', ('ctx', 'dp'))
The draws below stay inside these ranges and needn't reach their ends.
Inputs may be any that keep to these rules, and one draw needn't show every extreme that they name: `segments`: within each sequence the ids never fall and each segment holds 1 to 1024 tokens.
All inputs are finite; a program needn't handle non-finite values.
Results may differ from the reference program's by a relative error of at most 0.006.
Values may be sent and summed in bfloat16 or wider, within the bound.
A program may use at most 64 MiB of HBM per device.

```python
import math
import jax
import jax.numpy as jnp
import numpy as np
from jax import lax

D = 1024
H = 4
DH = 128
SEGS = 4
SEQ = 2048
MOST = 1024
P_SIZE = 524288
N_PIPE = 8
N_CTX = 8
N_DP = 16


def draw_w_qkv(key, part):
    head_cols = H * DH
    normal_part = jax.random.normal(key, (N_PIPE, D, 3 * head_cols), jnp.float32) * D ** (-0.5)
    return normal_part.astype(jnp.bfloat16)


def with_spikes(drawn, own_key, source, target, blocks, factor):
    owner, partner = [(jnp.arange(drawn.shape[dim]) // (drawn.shape[dim] // blocks)).reshape([-1 if axis == dim else 1 for axis in range(drawn.ndim)]) for dim in (source, target)]
    chosen = jax.random.permutation(own_key, blocks)[partner]
    strong = (owner == chosen) | (owner == (partner + blocks // 2) % blocks)
    return jnp.where(strong, factor * drawn, drawn)


def block_scale(own_key, dims, cuts, smallest, largest):
    gain = 1.0
    for position, parts in cuts:
        heights = jax.random.uniform(jax.random.fold_in(jax.random.fold_in(own_key, 6), position), (parts,), jnp.float32, smallest / len(cuts), largest / len(cuts))
        gain = gain * jnp.repeat(jnp.exp(heights), dims[position] // parts).reshape((-1,) + (1,) * (len(dims) - 1 - position))
    return gain


def split_up(count, total, limit, lean):
    weights = [(1 << 20) // math.isqrt(rank ** lean) + 1 for rank in range(2, count + 1)]
    surplus, holding = total - limit - (count - 1), [1] * (count - 1)
    while surplus > 0:
        free = [i for i in range(count - 1) if holding[i] < limit]
        pool, left = sum([weights[i] for i in free]), surplus
        for i in free:
            extra = min(limit - holding[i], max(1, left * weights[i] // pool), surplus)
            holding[i] = holding[i] + extra
            surplus = surplus - extra
    return np.array([limit] + holding)


def ragged(stream_key, amount, total, bound, lean):
    if amount == 2:
        one = jax.random.randint(stream_key, (), max(1, total - bound), min(bound, total - 1) + 1)
        return jnp.stack([one, total - one])
    sizes = jnp.asarray(split_up(amount, total, bound, lean), jnp.int32)
    twos = (amount - 1) // 2
    giver, sink = sizes[1:1 + 2 * twos:2], sizes[2:2 + 2 * twos:2]
    margin = jnp.minimum(giver - 1, bound - sink)
    moved = jax.random.randint(jax.random.fold_in(stream_key, 1), (twos,), 0, 1 << 20) % (margin + 1)
    sizes = sizes.at[1:1 + 2 * twos:2].set(giver - moved).at[2:2 + 2 * twos:2].set(sink + moved)
    return sizes[jax.random.permutation(jax.random.fold_in(stream_key, 2), amount)]


def noise(key, shape, width, limit, shards=(), kind=jnp.bfloat16):
    values = width * jax.random.normal(key, shape, jnp.float32)
    if shards:
        values = values * block_scale(key, shape, shards, -0.22, 0.18)
    return jnp.clip(values, -limit, limit).astype(kind)


def noise_with(key, shape, width, reach, shards, heavy, kind=jnp.bfloat16):
    drawn = width * jax.random.normal(key, shape, jnp.float32)
    if shards:
        drawn = drawn * block_scale(key, shape, shards, -0.22, 0.18)
    return jnp.clip(with_spikes(drawn, jax.random.fold_in(key, 3), *heavy), -reach, reach).astype(kind)


def setup_inputs(seed: int = 0) -> dict:
    keys = jax.random.split(jax.random.key(seed), 10)
    return {
        "section_held": noise(keys[0], (N_PIPE, N_DP, SEQ, D), 1.0, 6.0, ((0, 8), (1, 16), (2, 8))),
        "segments": jax.vmap(lambda own: jnp.searchsorted(jnp.cumsum(ragged(own, SEGS, SEQ, MOST, 1)), jnp.arange(SEQ), side="right"))(jax.random.split(keys[1], N_PIPE * N_DP)).reshape((N_PIPE, N_DP, SEQ)).astype(jnp.int32),
        "norm_gain": jnp.clip(1.0 + 0.18 * jax.random.normal(keys[2], (N_PIPE, D), jnp.float32), 0.1, 1.9),
        "w_qkv": draw_w_qkv(jax.random.fold_in(keys[9], 71), 0),
        "w_out": noise(keys[4], (N_PIPE, H * DH, D), (H * DH // 16) ** -0.5, 1.0, ((0, 8),)),
        "grad_parts": noise_with(keys[5], (N_PIPE, N_CTX, N_DP, P_SIZE), 0.1, 2.0, ((0, 8), (1, 8), (2, 16)), (2, 3, 16, 2.0), jnp.float32),
        "master": noise(keys[6], (N_PIPE, P_SIZE), (H * DH) ** -0.5, 0.25, ((0, 8), (1, 128)), jnp.float32),
        "moment": noise(keys[7], (N_PIPE, P_SIZE), 0.3, 4.0, ((0, 8), (1, 128)), jnp.float32),
        "second": jnp.clip(jnp.exp(math.log(1.0) - 2.3025851 * jax.random.uniform(keys[8], (N_PIPE, P_SIZE), jnp.float32) ** block_scale(keys[8], (N_PIPE, P_SIZE), ((0, 8), (1, 128)), -0.2, 0.2)), 0.1, 1.0),
    }


eps_norm = 1e-06
rate = 0.001
beta_one = 0.9
beta_two = 0.999
adam_eps = 1e-08
decay = 0.1
fix_one = 0.9999734386011124
fix_two = 0.09520785288629038

def attend_layer(inputs, seg_ids, gain_row, proj_in, proj_out):
    head_cols = H * DH
    seq_len = inputs.shape[0]
    values = inputs.astype(jnp.float32)
    meansq = lax.optimization_barrier(jnp.mean(values * values, axis=-1, keepdims=True))
    normed = (values * lax.rsqrt(meansq + eps_norm) * gain_row).astype(jnp.bfloat16)
    projected = jnp.dot(normed, proj_in, preferred_element_type=jnp.float32)
    queries = projected[:, :head_cols].astype(jnp.bfloat16).reshape(seq_len, H, DH)
    key_rows = projected[:, head_cols:2 * head_cols].astype(jnp.bfloat16).reshape(seq_len, H, DH)
    value_rows = projected[:, 2 * head_cols:].astype(jnp.bfloat16).reshape(seq_len, H, DH)
    scores = jnp.einsum('qhd,khd->hqk', queries.astype(jnp.float32), key_rows.astype(jnp.float32)) * DH ** (-0.5)
    places = jnp.arange(seq_len, dtype=jnp.int32)
    allowed = (places[None, :] <= places[:, None]) & (seg_ids[None, :] == seg_ids[:, None])
    scores = jnp.where(allowed[None], scores, -1e+30)
    row_top = lax.optimization_barrier(jnp.max(scores, axis=-1, keepdims=True))
    weights = jnp.where(allowed[None], jnp.exp(scores - row_top), 0.0)
    totals = lax.optimization_barrier(jnp.sum(weights, axis=-1))
    rounded = lax.optimization_barrier(weights.astype(jnp.bfloat16)).astype(jnp.float32)
    summed = jnp.einsum('hqk,khd->qhd', rounded, value_rows.astype(jnp.float32))
    attended = (summed / jnp.transpose(totals)[:, :, None]).reshape(seq_len, head_cols).astype(jnp.bfloat16)
    return (jnp.dot(attended, proj_out, preferred_element_type=jnp.float32) + values).astype(jnp.bfloat16)

def reference(section_held, segments, norm_gain, w_qkv, w_out, grad_parts, master, moment, second):
    incoming = jnp.roll(section_held, 1, axis=0)
    flat_in = incoming.reshape(N_PIPE * N_DP, SEQ, D)
    flat_seg = segments.reshape(N_PIPE * N_DP, SEQ)
    section_ids = (jnp.arange(N_PIPE * N_DP) // N_DP).astype(jnp.int32)

    def per_sequence(element):
        inputs, seg_ids, section_id = element
        return attend_layer(inputs, seg_ids, norm_gain[section_id], w_qkv[section_id], w_out[section_id])
    outputs = lax.map(per_sequence, (flat_in, flat_seg, section_ids)).reshape(section_held.shape)
    grad_sum = lax.optimization_barrier(jnp.sum(grad_parts, axis=(1, 2)))
    new_moment = beta_one * moment + (1.0 - beta_one) * grad_sum
    new_second = beta_two * second + (1.0 - beta_two) * grad_sum * grad_sum
    update = new_moment / fix_one / (jnp.sqrt(new_second / fix_two) + adam_eps) + decay * master
    new_master = master - rate * update
    return (outputs, new_master, new_moment, new_second)
```

```python
import functools

import jax
import jax.numpy as jnp
from jax import lax
from jax.experimental import pallas as pl
from jax.experimental.pallas import tpu as pltpu
from jax.sharding import PartitionSpec as P

H = 4
DH = 128
D = 1024
ROWS = 256
HALF = 128
HC = H * DH
FAR = 4
NEG = -1e30

eps_norm = 1e-06
rate = 0.001
beta_one = 0.9
beta_two = 0.999
adam_eps = 1e-08
decay = 0.1
fix_one = 0.9999734386011124
fix_two = 0.09520785288629038

MESH = pl.DeviceIdType.MESH
F32 = jnp.float32
BF16 = jnp.bfloat16


def kernel(
    x_hbm, seg_hbm, gain_hbm, wqkv_hbm, wout_hbm, g_hbm, ma_hbm, mo_hbm, se_hbm,
    out_hbm, nma_hbm, nmo_hbm, nse_hbm,
    xin, nrm, wqkv, wout, gain, seg, segq, kv, qs, acc, ms, ls, ov,
    g, r1a, r1b, r2p, r2m, red, rp, rm, ma, mo, se,
    loc, osem, xs, xr, ys, yr, ks, kr, zps, zpr, zms, zmr,
):
    p, c, d = lax.axis_index("pipe"), lax.axis_index("ctx"), lax.axis_index("dp")
    zh, y = lax.div(d, 4), lax.rem(d, 4)
    z = zh * 8 + c
    yp, ym, y2 = lax.rem(y + 1, 4), lax.rem(y + 3, 4), lax.rem(y + 2, 4)
    nxt, prv = (lax.rem(p + 1, 8), c, d), (lax.rem(p + 7, 8), c, d)
    dev_yp, dev_ym = (p, c, zh * 4 + yp), (p, c, zh * 4 + ym)
    up = (p, lax.rem(c + 1, 8), lax.rem(zh + lax.div(c + 1, 8), 4) * 4 + y)
    down = (p, lax.rem(c + 7, 8), lax.rem(zh + 3 + lax.div(c + 7, 8), 4) * 4 + y)

    def remote(src, dst, ssem, rsem, dev):
        return pltpu.make_async_remote_copy(
            src_ref=src, dst_ref=dst, send_sem=ssem, recv_sem=rsem, device_id=dev, device_id_type=MESH
        )

    local = [
        pltpu.make_async_copy(a, b, loc.at[i])
        for i, (a, b) in enumerate(
            [(seg_hbm, seg), (gain_hbm, gain), (wqkv_hbm, wqkv), (g_hbm, g), (wout_hbm, wout),
             (ma_hbm, ma), (mo_hbm, mo), (se_hbm, se)]
        )
    ]
    for one in local:
        one.start()

    barrier = pltpu.get_barrier_semaphore()
    for dev in (nxt, prv, dev_yp, dev_ym, up, down):
        pl.semaphore_signal(barrier, inc=1, device_id=dev, device_id_type=MESH)
    pl.semaphore_wait(barrier, 6)

    def x_copy(r):
        rows = pl.ds(r * HALF, HALF)
        return remote(x_hbm.at[rows], xin.at[rows], xs.at[r], xr.at[r], nxt)

    y_one = [
        remote(g_hbm.at[pl.ds(0, 4), :, y2], r1a, ys.at[0], yr.at[0], dev_yp),
        remote(g_hbm.at[pl.ds(4, 4), :, y2], r1b, ys.at[1], yr.at[1], dev_ym),
    ]
    y_two = [
        remote(g_hbm.at[pl.ds(4, 4), :, yp], r2p.at[pl.ds(4, 4)], ys.at[2], yr.at[2], dev_yp),
        remote(g_hbm.at[pl.ds(0, 4), :, ym], r2m.at[pl.ds(0, 4)], ys.at[3], yr.at[3], dev_ym),
    ]
    y_sum = [
        remote(r1a, r2p.at[pl.ds(0, 4)], ys.at[4], yr.at[4], dev_yp),
        remote(r1b, r2m.at[pl.ds(4, 4)], ys.at[5], yr.at[5], dev_ym),
    ]
    for r in range(2):
        x_copy(r).start()
    for one in (*y_one, *y_two):
        one.start()

    def kv_copy(k, r):
        return remote(kv.at[k, r], kv.at[k + 1, r], ks.at[k, r], kr.at[k, r], up)

    def project(r):
        rows = pl.ds(r * HALF, HALF)
        x_copy(r).wait_recv()
        values = xin[rows, :].astype(F32)
        meansq = jnp.mean(values * values, axis=-1, keepdims=True)
        normed = (values * lax.rsqrt(meansq + eps_norm) * gain[...]).astype(BF16)
        nrm[rows, :] = normed
        both = jnp.dot(normed, wqkv[:, HC:], preferred_element_type=F32).astype(BF16)
        for t in range(2):
            for h in range(H):
                kv[0, r, t, h] = both[:, t * HC + h * DH : t * HC + (h + 1) * DH]

        @pl.when(c < 7)
        def _():
            kv_copy(0, r).start()


    def attend(k, r, q0, qn, causal=False):
        rows = pl.ds(q0, qn)
        keyseg = seg[pl.ds(2 * (c - k) + r, 1), :]
        mask = segq[rows, :] == keyseg
        if causal:
            place = lax.broadcasted_iota(jnp.int32, (qn, HALF), 0) + q0
            mask = mask & (lax.broadcasted_iota(jnp.int32, (qn, HALF), 1) + r * HALF <= place)
        for h in range(H):
            s = lax.dot_general(
                qs[h, rows, :], kv[k, r, 0, h], (((1,), (1,)), ((), ())), preferred_element_type=F32
            )
            s = jnp.where(mask, s * (DH ** (-0.5)), NEG)
            old = ms[h, rows, :]
            top = jnp.maximum(old, jnp.max(s, axis=-1, keepdims=True))
            w = jnp.exp(s - top)
            shrink = jnp.exp(old - top)
            ms[h, rows, :] = top
            ls[h, rows, :] = shrink * ls[h, rows, :] + jnp.sum(w, axis=-1, keepdims=True)
            acc[h, rows, :] = shrink * acc[h, rows, :] + jnp.dot(
                w.astype(BF16), kv[k, r, 1, h], preferred_element_type=F32
            )

    def arrived(k, r):
        @pl.when(c >= k)
        def _():
            kv_copy(k - 1, r).wait_recv()

        if k < FAR:
            @pl.when((c >= k) & (c < 7))
            def _():
                kv_copy(k, r).start()

        @pl.when(c >= k)
        def _():
            if k == FAR and r == 0:
                attend(k, r, 0, HALF)
            else:
                attend(k, r, 0, ROWS)

    def shard(t):
        return lax.rem(t, 8), lax.div(t, 8)

    def up_copy(i):
        if i == 0:
            a, b = shard(lax.rem(z + 16, 32))
            src = red.at[a, b]
        else:
            src = rp.at[i - 1]
        return remote(src, rp.at[i], zps.at[i], zpr.at[i], up)

    def down_copy(i):
        if i == 0:
            a, b = shard(lax.rem(z + 17, 32))
            src = red.at[a, b]
        else:
            src = rm.at[i - 1]
        return remote(src, rm.at[i], zms.at[i], zmr.at[i], down)

    def ring(i):
        up_copy(i - 1).wait_recv()
        a, b = shard(lax.rem(z + 16 - i + 32, 32))
        rp[i - 1] = rp[i - 1] + red[a, b]
        up_copy(i).start()
        if i < 15:
            down_copy(i - 1).wait_recv()
            a, b = shard(lax.rem(z + 17 + i, 32))
            rm[i - 1] = rm[i - 1] + red[a, b]
            down_copy(i).start()

    for i in (0, 1, 2):
        local[i].wait()
    project(0)
    for r in range(2):
        cols = jnp.broadcast_to(seg[pl.ds(2 * c + r, 1), :], (HALF, HALF))
        segq[pl.ds(r * HALF, HALF), :] = jnp.transpose(cols)
    project(1)
    local[3].wait()
    y_one[0].wait_recv()
    r1a[...] = r1a[...] + g[pl.ds(0, 4), :, yp]
    y_sum[0].start()
    y_one[1].wait_recv()
    r1b[...] = r1b[...] + g[pl.ds(4, 4), :, ym]
    y_sum[1].start()

    queries = jnp.dot(nrm[...], wqkv[:, :HC], preferred_element_type=F32).astype(BF16)
    for h in range(H):
        qs[h] = queries[:, h * DH : (h + 1) * DH]
    ms[...] = jnp.full_like(ms, NEG)
    ls[...] = jnp.zeros_like(ls)
    acc[...] = jnp.zeros_like(acc)
    attend(0, 0, 0, ROWS, causal=True)
    attend(0, 1, HALF, HALF, causal=True)
    arrived(1, 0)

    for one in (*y_two, *y_sum):
        one.wait_recv()
    red[...] = g[:, :, y] + r2p[...] + r2m[...]
    up_copy(0).start()
    down_copy(0).start()
    arrived(1, 1)
    plan = {3: (2, 0), 6: (2, 1), 9: (3, 0), 12: (3, 1)}
    for i in range(1, 16):
        ring(i)
        if i in plan:
            arrived(*plan[i])
    for i in (5, 6, 7):
        local[i].wait()
    up_copy(15).wait_recv()
    down_copy(14).wait_recv()
    grad = red[c, zh] + rp[15] + rm[14]
    new_moment = beta_one * mo[...] + (1.0 - beta_one) * grad
    new_second = beta_two * se[...] + (1.0 - beta_two) * grad * grad
    update = new_moment / fix_one / (jnp.sqrt(new_second / fix_two) + adam_eps) + decay * ma[...]
    ma[...] = ma[...] - rate * update
    mo[...] = new_moment
    se[...] = new_second
    outs = [
        pltpu.make_async_copy(a, b, osem.at[i])
        for i, (a, b) in enumerate([(ma, nma_hbm), (mo, nmo_hbm), (se, nse_hbm), (ov, out_hbm)])
    ]
    for one in outs[:3]:
        one.start()
    local[4].wait()
    arrived(4, 0)
    arrived(4, 1)

    heads = [(acc[h] / ls[h]).astype(BF16) for h in range(H)]
    attended = jnp.concatenate(heads, axis=1)
    final = jnp.dot(attended, wout[...], preferred_element_type=F32) + xin[...].astype(F32)
    ov[...] = final.astype(BF16)
    outs[3].start()

    for r in range(2):
        x_copy(r).wait_send()
    for one in (*y_one, *y_two, *y_sum):
        one.wait_send()
    for i in range(16):
        up_copy(i).wait_send()
    for i in range(15):
        down_copy(i).wait_send()
    for k in range(FAR):
        @pl.when((c >= k) & (c < 7))
        def _():
            for r in range(2):
                kv_copy(k, r).wait_send()
    for one in outs:
        one.wait()


def on_device(section_held, segments, norm_gain, w_qkv, w_out, grad_parts, master, moment, second):
    shard_rows = (32, 128)
    any_spec = pl.BlockSpec(memory_space=pl.ANY)
    vmem, dma = pltpu.VMEM, pltpu.SemaphoreType.DMA
    outs = pl.pallas_call(
        kernel,
        out_shape=(
            jax.ShapeDtypeStruct((ROWS, D), BF16),
            jax.ShapeDtypeStruct(shard_rows, F32),
            jax.ShapeDtypeStruct(shard_rows, F32),
            jax.ShapeDtypeStruct(shard_rows, F32),
        ),
        in_specs=[any_spec] * 9,
        out_specs=[any_spec] * 4,
        scratch_shapes=[
            vmem((ROWS, D), BF16),
            vmem((ROWS, D), BF16),
            vmem((D, 3 * HC), BF16),
            vmem((HC, D), BF16),
            vmem((1, D), F32),
            vmem((16, 128), jnp.int32),
            vmem((ROWS, HALF), jnp.int32),
            vmem((FAR + 1, 2, 2, H, HALF, DH), BF16),
            vmem((H, ROWS, DH), BF16),
            vmem((H, ROWS, DH), F32),
            vmem((H, ROWS, DH), F32),
            vmem((H, ROWS, DH), F32),
            vmem((ROWS, D), BF16),
            vmem((8, 4, 4, 32, 128), F32),
            vmem((4, 4, 32, 128), F32),
            vmem((4, 4, 32, 128), F32),
            vmem((8, 4, 32, 128), F32),
            vmem((8, 4, 32, 128), F32),
            vmem((8, 4, 32, 128), F32),
            vmem((16, 32, 128), F32),
            vmem((15, 32, 128), F32),
            vmem(shard_rows, F32),
            vmem(shard_rows, F32),
            vmem(shard_rows, F32),
            dma((8,)), dma((4,)),
            dma((2,)), dma((2,)),
            dma((6,)), dma((6,)),
            dma((FAR, 2)), dma((FAR, 2)),
            dma((16,)), dma((16,)),
            dma((15,)), dma((15,)),
        ],
        compiler_params=pltpu.CompilerParams(
            collective_id=0, has_side_effects=True, vmem_limit_bytes=48 << 20
        ),
    )(
        section_held.reshape(ROWS, D),
        segments.reshape(16, 128),
        norm_gain,
        w_qkv[0],
        w_out[0],
        grad_parts.reshape(8, 4, 4, 32, 128),
        master.reshape(shard_rows),
        moment.reshape(shard_rows),
        second.reshape(shard_rows),
    )
    return (
        outs[0].reshape(section_held.shape),
        outs[1].reshape(master.shape),
        outs[2].reshape(moment.shape),
        outs[3].reshape(second.shape),
    )


def solution(mesh):
    in_specs = (
        P("pipe", "dp", "ctx", None),
        P("pipe", "dp", None),
        P("pipe", None),
        P("pipe", None, None),
        P("pipe", None, None),
        P("pipe", "ctx", "dp", None),
        P("pipe", ("ctx", "dp")),
        P("pipe", ("ctx", "dp")),
        P("pipe", ("ctx", "dp")),
    )
    out_specs = (
        P("pipe", "dp", "ctx", None),
        P("pipe", ("ctx", "dp")),
        P("pipe", ("ctx", "dp")),
        P("pipe", ("ctx", "dp")),
    )
    return jax.shard_map(
        on_device, mesh=mesh, in_specs=in_specs, out_specs=out_specs, check_vma=False
    )
```

```python
import functools

import jax
import jax.numpy as jnp
from jax import lax
from jax.experimental import pallas as pl
from jax.experimental.pallas import tpu as pltpu
from jax.sharding import PartitionSpec as P

H = 4
DH = 128
D = 1024
ROWS = 256
HALF = 128
HC = H * DH
FAR_ORDER = (4, 3, 5, 2, 6, 1, 7)
FAR = 4
NEG = -1e30

eps_norm = 1e-06
rate = 0.001
beta_one = 0.9
beta_two = 0.999
adam_eps = 1e-08
decay = 0.1
fix_one = 0.9999734386011124
fix_two = 0.09520785288629038

MESH = pl.DeviceIdType.MESH
F32 = jnp.float32
BF16 = jnp.bfloat16


def kernel(
    x_hbm, seg_hbm, gain_hbm, wqkv_hbm, wout_hbm, g_hbm, ma_hbm, mo_hbm, se_hbm,
    ov, nma, nmo, nse,
    xin, nrm, wqkv, wout, gain, seg, segq, kv, qs, acc, ms, ls,
    g, yin, red, win, far, ma, mo, se,
    loc, xs, xr, ys, yr, ks, kr, ws, wr, fs, fr,
):
    p, c, d = lax.axis_index("pipe"), lax.axis_index("ctx"), lax.axis_index("dp")
    zh, y = lax.div(d, 4), lax.rem(d, 4)
    z = zh * 8 + c
    nxt, prv = (lax.rem(p + 1, 8), c, d), (lax.rem(p + 7, 8), c, d)

    def along_y(by):
        return p, c, zh * 4 + lax.rem(y + by, 4)

    def along_z(by):
        at = lax.rem(z + by + 32, 32)
        return p, lax.rem(at, 8), lax.div(at, 8) * 4 + y

    up = along_z(1)

    def remote(src, dst, ssem, rsem, dev):
        return pltpu.make_async_remote_copy(
            src_ref=src, dst_ref=dst, send_sem=ssem, recv_sem=rsem, device_id=dev, device_id_type=MESH
        )

    local = [
        pltpu.make_async_copy(a, b, loc.at[i])
        for i, (a, b) in enumerate(
            [(seg_hbm, seg), (gain_hbm, gain), (wqkv_hbm, wqkv), (g_hbm, g), (wout_hbm, wout),
             (ma_hbm, ma), (mo_hbm, mo), (se_hbm, se)]
        )
    ]
    for one in local:
        one.start()

    barrier = pltpu.get_barrier_semaphore()
    peers = [nxt, prv] + [along_y(i) for i in (1, 2, 3)]
    peers += [along_z(i) for i in (1, 2, 3, -1, -2, -3)] + [along_z(4 * i) for i in range(1, 8)]
    for dev in peers:
        pl.semaphore_signal(barrier, inc=1, device_id=dev, device_id_type=MESH)
    pl.semaphore_wait(barrier, len(peers))

    def x_copy(r):
        rows = pl.ds(r * HALF, HALF)
        return remote(x_hbm.at[rows], xin.at[rows], xs.at[r], xr.at[r], nxt)

    def group(j):
        return lax.rem(z + 1 + j, 4)

    def y_copy(j, i):
        src = g_hbm.at[:, group(j), :, lax.rem(y + i, 4)]
        return remote(src, yin.at[j, i - 1], ys.at[j, i - 1], yr.at[j, i - 1], along_y(i))

    for r in range(2):
        x_copy(r).start()
    for j in range(4):
        for i in (1, 2, 3):
            y_copy(j, i).start()

    def kv_copy(k, r):
        return remote(kv.at[k, r], kv.at[k + 1, r], ks.at[k, r], kr.at[k, r], up)

    def project(r):
        rows = pl.ds(r * HALF, HALF)
        x_copy(r).wait_recv()
        values = xin[rows, :].astype(F32)
        meansq = jnp.mean(values * values, axis=-1, keepdims=True)
        normed = (values * lax.rsqrt(meansq + eps_norm) * gain[...]).astype(BF16)
        nrm[rows, :] = normed
        both = jnp.dot(normed, wqkv[:, HC:], preferred_element_type=F32).astype(BF16)
        for t in range(2):
            for h in range(H):
                kv[0, r, t, h] = both[:, t * HC + h * DH : t * HC + (h + 1) * DH]

        @pl.when(c < 7)
        def _():
            kv_copy(0, r).start()


    def attend(k, r, q0, qn, causal=False):
        rows = pl.ds(q0, qn)
        keyseg = seg[pl.ds(2 * (c - k) + r, 1), :]
        mask = segq[rows, :] == keyseg
        if causal:
            place = lax.broadcasted_iota(jnp.int32, (qn, HALF), 0) + q0
            mask = mask & (lax.broadcasted_iota(jnp.int32, (qn, HALF), 1) + r * HALF <= place)
        for h in range(H):
            s = lax.dot_general(
                qs[h, rows, :], kv[k, r, 0, h], (((1,), (1,)), ((), ())), preferred_element_type=F32
            )
            s = jnp.where(mask, s * (DH ** (-0.5)), NEG)
            old = ms[h, rows, :]
            top = jnp.maximum(old, jnp.max(s, axis=-1, keepdims=True))
            w = jnp.exp(s - top)
            shrink = jnp.exp(old - top)
            ms[h, rows, :] = top
            ls[h, rows, :] = shrink * ls[h, rows, :] + jnp.sum(w, axis=-1, keepdims=True)
            acc[h, rows, :] = shrink * acc[h, rows, :] + jnp.dot(
                w.astype(BF16), kv[k, r, 1, h], preferred_element_type=F32
            )

    def arrived(k, r):
        @pl.when(c >= k)
        def _():
            kv_copy(k - 1, r).wait_recv()

        if k < FAR:
            @pl.when((c >= k) & (c < 7))
            def _():
                kv_copy(k, r).start()

        @pl.when(c >= k)
        def _():
            if k == FAR and r == 0:
                attend(k, r, 0, HALF)
            else:
                attend(k, r, 0, ROWS)

    def w_copy(j):
        return remote(red.at[j], win.at[j], ws.at[j], wr.at[j], along_z(j - 3))

    def y_sum(j):
        for i in (1, 2, 3):
            y_copy(j, i).wait_recv()
        red[j] = g[:, group(j), :, y] + yin[j, 0] + yin[j, 1] + yin[j, 2]
        if j < 3:
            w_copy(j).start()

    def f_copy(i):
        at = lax.rem(z + 32 - 4 * i, 32)
        src = red.at[3, lax.div(lax.rem(at, 8), 4), lax.div(at, 8)]
        return remote(src, far.at[i - 1], fs.at[i - 1], fr.at[i - 1], along_z(-4 * i))

    def w_sum():
        for j in range(3):
            w_copy(j).wait_recv()
        red[3] = red[3] + win[0] + win[1] + win[2]
        for i in FAR_ORDER:
            f_copy(i).start()

    for i in (0, 1, 2):
        local[i].wait()
    project(0)
    for r in range(2):
        cols = jnp.broadcast_to(seg[pl.ds(2 * c + r, 1), :], (HALF, HALF))
        segq[pl.ds(r * HALF, HALF), :] = jnp.transpose(cols)
    project(1)
    queries = jnp.dot(nrm[...], wqkv[:, :HC], preferred_element_type=F32).astype(BF16)
    for h in range(H):
        qs[h] = queries[:, h * DH : (h + 1) * DH]
    local[3].wait()
    y_sum(0)
    ms[...] = jnp.full_like(ms, NEG)
    ls[...] = jnp.zeros_like(ls)
    acc[...] = jnp.zeros_like(acc)
    attend(0, 0, 0, ROWS, causal=True)
    attend(0, 1, HALF, HALF, causal=True)
    arrived(1, 0)
    y_sum(1)
    arrived(1, 1)
    y_sum(2)
    arrived(2, 0)
    y_sum(3)
    arrived(2, 1)
    w_sum()
    arrived(3, 0)
    arrived(3, 1)
    arrived(4, 0)
    for i in (5, 6, 7):
        local[i].wait()
    for i in range(1, 8):
        f_copy(i).wait_recv()
    grad = red[3, lax.div(c, 4), zh]
    for i in range(7):
        grad = grad + far[i]
    new_moment = beta_one * mo[...] + (1.0 - beta_one) * grad
    new_second = beta_two * se[...] + (1.0 - beta_two) * grad * grad
    update = new_moment / fix_one / (jnp.sqrt(new_second / fix_two) + adam_eps) + decay * ma[...]
    nma[...] = ma[...] - rate * update
    nmo[...] = new_moment
    nse[...] = new_second
    local[4].wait()
    arrived(4, 1)

    heads = [(acc[h] / ls[h]).astype(BF16) for h in range(H)]
    attended = jnp.concatenate(heads, axis=1)
    final = jnp.dot(attended, wout[...], preferred_element_type=F32) + xin[...].astype(F32)
    ov[...] = final.astype(BF16)

    for r in range(2):
        x_copy(r).wait_send()
    for j in range(4):
        for i in (1, 2, 3):
            y_copy(j, i).wait_send()
    for j in range(3):
        w_copy(j).wait_send()
    for i in range(1, 8):
        f_copy(i).wait_send()
    for k in range(FAR):
        @pl.when((c >= k) & (c < 7))
        def _():
            for r in range(2):
                kv_copy(k, r).wait_send()


def hand_over(*refs):
    sems = refs[8]
    copies = [pltpu.make_async_copy(refs[i], refs[4 + i], sems.at[i]) for i in range(4)]
    for one in copies:
        one.start()
    for one in copies:
        one.wait()


def on_device(section_held, segments, norm_gain, w_qkv, w_out, grad_parts, master, moment, second):
    shard_rows = (32, 128)
    any_spec = pl.BlockSpec(memory_space=pl.ANY)
    vmem_spec = pl.BlockSpec(memory_space=pltpu.VMEM)
    vmem, dma = pltpu.VMEM, pltpu.SemaphoreType.DMA
    outs = pl.pallas_call(
        kernel,
        out_shape=(
            vmem((ROWS, D), BF16),
            vmem(shard_rows, F32),
            vmem(shard_rows, F32),
            vmem(shard_rows, F32),
        ),
        in_specs=[pl.BlockSpec(memory_space=pltpu.HBM)] * 9,
        out_specs=[vmem_spec] * 4,
        scratch_shapes=[
            vmem((ROWS, D), BF16),
            vmem((ROWS, D), BF16),
            vmem((D, 3 * HC), BF16),
            vmem((HC, D), BF16),
            vmem((1, D), F32),
            vmem((16, 128), jnp.int32),
            vmem((ROWS, HALF), jnp.int32),
            vmem((FAR + 1, 2, 2, H, HALF, DH), BF16),
            vmem((H, ROWS, DH), BF16),
            vmem((H, ROWS, DH), F32),
            vmem((H, ROWS, DH), F32),
            vmem((H, ROWS, DH), F32),
            vmem((2, 4, 4, 4, 32, 128), F32),
            vmem((4, 3, 2, 4, 32, 128), F32),
            vmem((4, 2, 4, 32, 128), F32),
            vmem((3, 2, 4, 32, 128), F32),
            vmem((7, 32, 128), F32),
            vmem(shard_rows, F32),
            vmem(shard_rows, F32),
            vmem(shard_rows, F32),
            dma((8,)),
            dma((2,)), dma((2,)),
            dma((4, 3)), dma((4, 3)),
            dma((FAR, 2)), dma((FAR, 2)),
            dma((3,)), dma((3,)),
            dma((7,)), dma((7,)),
        ],
        compiler_params=pltpu.CompilerParams(
            collective_id=0, has_side_effects=True, vmem_limit_bytes=48 << 20
        ),
    )(
        *(pltpu.with_memory_space_constraint(one, pltpu.HBM) for one in (
            section_held.reshape(ROWS, D),
            segments.reshape(16, 128),
            norm_gain,
            w_qkv[0],
            w_out[0],
            grad_parts.reshape(2, 4, 4, 4, 32, 128),
            master.reshape(shard_rows),
            moment.reshape(shard_rows),
            second.reshape(shard_rows),
        ))
    )
    outs = pl.pallas_call(
        hand_over,
        out_shape=[jax.ShapeDtypeStruct(one.shape, one.dtype) for one in outs],
        in_specs=[any_spec] * 4,
        out_specs=[any_spec] * 4,
        scratch_shapes=[dma((4,))],
        compiler_params=pltpu.CompilerParams(vmem_limit_bytes=4 << 20),
    )(*outs)
    return (
        outs[0].reshape(section_held.shape),
        outs[1].reshape(master.shape),
        outs[2].reshape(moment.shape),
        outs[3].reshape(second.shape),
    )


def solution(mesh):
    in_specs = (
        P("pipe", "dp", "ctx", None),
        P("pipe", "dp", None),
        P("pipe", None),
        P("pipe", None, None),
        P("pipe", None, None),
        P("pipe", "ctx", "dp", None),
        P("pipe", ("ctx", "dp")),
        P("pipe", ("ctx", "dp")),
        P("pipe", ("ctx", "dp")),
    )
    out_specs = (
        P("pipe", "dp", "ctx", None),
        P("pipe", ("ctx", "dp")),
        P("pipe", ("ctx", "dp")),
        P("pipe", ("ctx", "dp")),
    )
    return jax.shard_map(
        on_device, mesh=mesh, in_specs=in_specs, out_specs=out_specs, check_vma=False
    )
```

```python
import functools

import jax
import jax.numpy as jnp
from jax import lax
from jax.experimental import pallas as pl
from jax.experimental.pallas import tpu as pltpu
from jax.sharding import PartitionSpec as P

H = 4
DH = 128
D = 1024
ROWS = 256
HALF = 128
HC = H * DH
FAR_ORDER = (4, 3, 5, 2, 6, 1, 7)
FAR = 4
NEG = -1e30

eps_norm = 1e-06
rate = 0.001
beta_one = 0.9
beta_two = 0.999
adam_eps = 1e-08
decay = 0.1
fix_one = 0.9999734386011124
fix_two = 0.09520785288629038

MESH = pl.DeviceIdType.MESH
F32 = jnp.float32
BF16 = jnp.bfloat16


def kernel(
    x_hbm, seg_hbm, gain_hbm, wqkv_hbm, wout_hbm, g_hbm, ma_hbm, mo_hbm, se_hbm,
    ov, nma, nmo, nse,
    xin, nrm, wqkv, wout, gain, seg, segq, kv, qs, acc, ms, ls,
    g, yin, red, win, far, ma, mo, se,
    loc, xs, xr, ys, yr, ks, kr, ws, wr, fs, fr, said,
):
    p, c, d = lax.axis_index("pipe"), lax.axis_index("ctx"), lax.axis_index("dp")
    zh, y = lax.div(d, 4), lax.rem(d, 4)
    z = zh * 8 + c
    nxt, prv = (lax.rem(p + 1, 8), c, d), (lax.rem(p + 7, 8), c, d)

    def along_y(by):
        return p, c, zh * 4 + lax.rem(y + by, 4)

    def along_z(by):
        at = lax.rem(z + by + 32, 32)
        return p, lax.rem(at, 8), lax.div(at, 8) * 4 + y

    up = along_z(1)

    def remote(src, dst, ssem, rsem, dev):
        return pltpu.make_async_remote_copy(
            src_ref=src, dst_ref=dst, send_sem=ssem, recv_sem=rsem, device_id=dev, device_id_type=MESH
        )

    local = [
        pltpu.make_async_copy(a, b, loc.at[i])
        for i, (a, b) in enumerate(
            [(seg_hbm, seg), (gain_hbm, gain), (wqkv_hbm, wqkv), (g_hbm, g), (wout_hbm, wout),
             (ma_hbm, ma), (mo_hbm, mo), (se_hbm, se)]
        )
    ]
    for one in local:
        one.start()

    barrier = pltpu.get_barrier_semaphore()
    for dev in (prv, along_y(1), along_y(2), along_y(3), along_z(-1)):
        pl.semaphore_signal(barrier, inc=1, device_id=dev, device_id_type=MESH)
    pl.semaphore_wait(barrier, 5)
    pl.semaphore_signal(said.at[0], inc=1, device_id=up, device_id_type=MESH)

    def known(i):
        pl.semaphore_wait(said.at[i], 1 if i == 0 else 2)
        if i < 6:
            far_by = 1 if i < 3 else 4
            for by in (far_by, -far_by):
                pl.semaphore_signal(said.at[i + 1], inc=1, device_id=along_z(by), device_id_type=MESH)

    def x_copy(r):
        rows = pl.ds(r * HALF, HALF)
        return remote(x_hbm.at[rows], xin.at[rows], xs.at[r], xr.at[r], nxt)

    def group(j):
        return lax.rem(z + 3 - j, 4)

    def y_copy(j, i):
        src = g_hbm.at[:, group(j), :, lax.rem(y + i, 4)]
        return remote(src, yin.at[j, i - 1], ys.at[j, i - 1], yr.at[j, i - 1], along_y(i))

    for r in range(2):
        x_copy(r).start()
    for j in range(4):
        for i in (1, 2, 3):
            y_copy(j, i).start()

    def kv_copy(k, r):
        return remote(kv.at[k, r], kv.at[k + 1, r], ks.at[k, r], kr.at[k, r], up)

    def project(r):
        rows = pl.ds(r * HALF, HALF)
        x_copy(r).wait_recv()
        values = xin[rows, :].astype(F32)
        meansq = jnp.mean(values * values, axis=-1, keepdims=True)
        normed = (values * lax.rsqrt(meansq + eps_norm) * gain[...]).astype(BF16)
        nrm[rows, :] = normed
        both = jnp.dot(normed, wqkv[:, HC:], preferred_element_type=F32).astype(BF16)
        for t in range(2):
            for h in range(H):
                kv[0, r, t, h] = both[:, t * HC + h * DH : t * HC + (h + 1) * DH]

        @pl.when(c < 7)
        def _():
            kv_copy(0, r).start()


    def attend(k, r, q0, qn, causal=False):
        rows = pl.ds(q0, qn)
        keyseg = seg[pl.ds(2 * (c - k) + r, 1), :]
        mask = segq[rows, :] == keyseg
        if causal:
            place = lax.broadcasted_iota(jnp.int32, (qn, HALF), 0) + q0
            mask = mask & (lax.broadcasted_iota(jnp.int32, (qn, HALF), 1) + r * HALF <= place)
        for h in range(H):
            s = lax.dot_general(
                qs[h, rows, :], kv[k, r, 0, h], (((1,), (1,)), ((), ())), preferred_element_type=F32
            )
            s = jnp.where(mask, s * (DH ** (-0.5)), NEG)
            old = ms[h, rows, :]
            top = jnp.maximum(old, jnp.max(s, axis=-1, keepdims=True))
            w = jnp.exp(s - top)
            shrink = jnp.exp(old - top)
            ms[h, rows, :] = top
            ls[h, rows, :] = shrink * ls[h, rows, :] + jnp.sum(w, axis=-1, keepdims=True)
            acc[h, rows, :] = shrink * acc[h, rows, :] + jnp.dot(
                w.astype(BF16), kv[k, r, 1, h], preferred_element_type=F32
            )

    def arrived(k, r):
        @pl.when(c >= k)
        def _():
            kv_copy(k - 1, r).wait_recv()

        if k < FAR:
            @pl.when((c >= k) & (c < 7))
            def _():
                kv_copy(k, r).start()

        @pl.when(c >= k)
        def _():
            if k == FAR and r == 0:
                attend(k, r, 0, HALF)
            else:
                attend(k, r, 0, ROWS)

    def w_copy(j):
        return remote(red.at[j], win.at[j], ws.at[j], wr.at[j], along_z(-1 - j))

    def y_sum(j):
        for i in (1, 2, 3):
            y_copy(j, i).wait_recv()
        red[j] = g[:, group(j), :, y] + yin[j, 0] + yin[j, 1] + yin[j, 2]
        if j < 3:
            w_copy(j).start()

    def f_copy(i):
        at = lax.rem(z + 32 - 4 * i, 32)
        src = red.at[3, lax.div(lax.rem(at, 8), 4), lax.div(at, 8)]
        return remote(src, far.at[i - 1], fs.at[i - 1], fr.at[i - 1], along_z(-4 * i))

    def w_sum():
        for j in range(3):
            w_copy(j).wait_recv()
        red[3] = red[3] + win[0] + win[1] + win[2]
        for i in FAR_ORDER:
            f_copy(i).start()

    for i in (0, 1, 2):
        local[i].wait()
    project(0)
    for r in range(2):
        cols = jnp.broadcast_to(seg[pl.ds(2 * c + r, 1), :], (HALF, HALF))
        segq[pl.ds(r * HALF, HALF), :] = jnp.transpose(cols)
    project(1)
    queries = jnp.dot(nrm[...], wqkv[:, :HC], preferred_element_type=F32).astype(BF16)
    for h in range(H):
        qs[h] = queries[:, h * DH : (h + 1) * DH]
    local[3].wait()
    ms[...] = jnp.full_like(ms, NEG)
    ls[...] = jnp.zeros_like(ls)
    acc[...] = jnp.zeros_like(acc)
    attend(0, 0, 0, ROWS, causal=True)
    attend(0, 1, HALF, HALF, causal=True)
    known(0)
    y_sum(0)
    arrived(1, 0)
    known(1)
    y_sum(1)
    arrived(1, 1)
    known(2)
    y_sum(2)
    arrived(2, 0)
    y_sum(3)
    known(3)
    known(4)
    arrived(2, 1)
    known(5)
    known(6)
    w_sum()
    arrived(3, 0)
    arrived(3, 1)
    arrived(4, 0)
    local[4].wait()
    arrived(4, 1)

    heads = [(acc[h] / ls[h]).astype(BF16) for h in range(H)]
    attended = jnp.concatenate(heads, axis=1)
    final = jnp.dot(attended, wout[...], preferred_element_type=F32) + xin[...].astype(F32)
    ov[...] = final.astype(BF16)

    for i in (5, 6, 7):
        local[i].wait()
    for i in range(1, 8):
        f_copy(i).wait_recv()
    grad = red[3, lax.div(c, 4), zh]
    for i in range(7):
        grad = grad + far[i]
    new_moment = beta_one * mo[...] + (1.0 - beta_one) * grad
    new_second = beta_two * se[...] + (1.0 - beta_two) * grad * grad
    update = new_moment / fix_one / (jnp.sqrt(new_second / fix_two) + adam_eps) + decay * ma[...]
    nma[...] = ma[...] - rate * update
    nmo[...] = new_moment
    nse[...] = new_second
    for r in range(2):
        x_copy(r).wait_send()
    for j in range(4):
        for i in (1, 2, 3):
            y_copy(j, i).wait_send()
    for j in range(3):
        w_copy(j).wait_send()
    for i in range(1, 8):
        f_copy(i).wait_send()
    for k in range(FAR):
        @pl.when((c >= k) & (c < 7))
        def _():
            for r in range(2):
                kv_copy(k, r).wait_send()


def hand_over(*refs):
    sems = refs[8]
    copies = [pltpu.make_async_copy(refs[i], refs[4 + i], sems.at[i]) for i in range(4)]
    for one in copies:
        one.start()
    for one in copies:
        one.wait()


def on_device(section_held, segments, norm_gain, w_qkv, w_out, grad_parts, master, moment, second):
    shard_rows = (32, 128)
    any_spec = pl.BlockSpec(memory_space=pl.ANY)
    vmem_spec = pl.BlockSpec(memory_space=pltpu.VMEM)
    vmem, dma = pltpu.VMEM, pltpu.SemaphoreType.DMA
    outs = pl.pallas_call(
        kernel,
        out_shape=(
            vmem((ROWS, D), BF16),
            vmem(shard_rows, F32),
            vmem(shard_rows, F32),
            vmem(shard_rows, F32),
        ),
        in_specs=[pl.BlockSpec(memory_space=pltpu.HBM)] * 9,
        out_specs=[vmem_spec] * 4,
        scratch_shapes=[
            vmem((ROWS, D), BF16),
            vmem((ROWS, D), BF16),
            vmem((D, 3 * HC), BF16),
            vmem((HC, D), BF16),
            vmem((1, D), F32),
            vmem((16, 128), jnp.int32),
            vmem((ROWS, HALF), jnp.int32),
            vmem((FAR + 1, 2, 2, H, HALF, DH), BF16),
            vmem((H, ROWS, DH), BF16),
            vmem((H, ROWS, DH), F32),
            vmem((H, ROWS, DH), F32),
            vmem((H, ROWS, DH), F32),
            vmem((2, 4, 4, 4, 32, 128), F32),
            vmem((4, 3, 2, 4, 32, 128), F32),
            vmem((4, 2, 4, 32, 128), F32),
            vmem((3, 2, 4, 32, 128), F32),
            vmem((7, 32, 128), F32),
            vmem(shard_rows, F32),
            vmem(shard_rows, F32),
            vmem(shard_rows, F32),
            dma((8,)),
            dma((2,)), dma((2,)),
            dma((4, 3)), dma((4, 3)),
            dma((FAR, 2)), dma((FAR, 2)),
            dma((3,)), dma((3,)),
            dma((7,)), dma((7,)),
            pltpu.SemaphoreType.REGULAR((7,)),
        ],
        compiler_params=pltpu.CompilerParams(
            collective_id=0, has_side_effects=True, vmem_limit_bytes=48 << 20
        ),
    )(
        *(pltpu.with_memory_space_constraint(one, pltpu.HBM) for one in (
            section_held.reshape(ROWS, D),
            segments.reshape(16, 128),
            norm_gain,
            w_qkv[0],
            w_out[0],
            grad_parts.reshape(2, 4, 4, 4, 32, 128),
            master.reshape(shard_rows),
            moment.reshape(shard_rows),
            second.reshape(shard_rows),
        ))
    )
    outs = pl.pallas_call(
        hand_over,
        out_shape=[jax.ShapeDtypeStruct(one.shape, one.dtype) for one in outs],
        in_specs=[any_spec] * 4,
        out_specs=[any_spec] * 4,
        scratch_shapes=[dma((4,))],
        compiler_params=pltpu.CompilerParams(vmem_limit_bytes=4 << 20),
    )(*outs)
    return (
        outs[0].reshape(section_held.shape),
        outs[1].reshape(master.shape),
        outs[2].reshape(moment.shape),
        outs[3].reshape(second.shape),
    )


def solution(mesh):
    in_specs = (
        P("pipe", "dp", "ctx", None),
        P("pipe", "dp", None),
        P("pipe", None),
        P("pipe", None, None),
        P("pipe", None, None),
        P("pipe", "ctx", "dp", None),
        P("pipe", ("ctx", "dp")),
        P("pipe", ("ctx", "dp")),
        P("pipe", ("ctx", "dp")),
    )
    out_specs = (
        P("pipe", "dp", "ctx", None),
        P("pipe", ("ctx", "dp")),
        P("pipe", ("ctx", "dp")),
        P("pipe", ("ctx", "dp")),
    )
    return jax.shard_map(
        on_device, mesh=mesh, in_specs=in_specs, out_specs=out_specs, check_vma=False
    )
```

```python
import functools

import jax
import jax.numpy as jnp
from jax import lax
from jax.experimental import pallas as pl
from jax.experimental.pallas import tpu as pltpu
from jax.sharding import PartitionSpec as P

H = 4
DH = 128
D = 1024
ROWS = 256
HALF = 128
HC = H * DH
NEG = -1e30

eps_norm = 1e-06
rate = 0.001
beta_one = 0.9
beta_two = 0.999
adam_eps = 1e-08
decay = 0.1
fix_one = 0.9999734386011124
fix_two = 0.09520785288629038

MESH = pl.DeviceIdType.MESH
F32 = jnp.float32
BF16 = jnp.bfloat16


def kernel(
    x_hbm, seg_hbm, gain_hbm, wqkv_hbm, wout_hbm, g_hbm, ma_hbm, mo_hbm, se_hbm,
    ov, nma, nmo, nse,
    xin, nrm, wqkv, wout, gain, seg, segk, segq, kv, qs, acc, ms, ls, part, stat,
    g, gb, yin, red, sent, win, far, ma, mo, se,
    loc, xs, xr, ys, yr, ks, kr, qss, qrs, ps, pr, ws, wr, fs, fr, said,
):
    p, c, d = lax.axis_index("pipe"), lax.axis_index("ctx"), lax.axis_index("dp")
    zh, y = lax.div(d, 4), lax.rem(d, 4)
    z = zh * 8 + c
    nxt, prv = (lax.rem(p + 1, 8), c, d), (lax.rem(p + 7, 8), c, d)

    def along_y(by):
        return p, c, zh * 4 + lax.rem(y + by, 4)

    def along_z(by):
        at = lax.rem(z + by + 32, 32)
        return p, lax.rem(at, 8), lax.div(at, 8) * 4 + y

    up, down = along_z(1), along_z(-1)

    def remote(src, dst, ssem, rsem, dev):
        return pltpu.make_async_remote_copy(
            src_ref=src, dst_ref=dst, send_sem=ssem, recv_sem=rsem, device_id=dev, device_id_type=MESH
        )

    local = [
        pltpu.make_async_copy(a, b, loc.at[i])
        for i, (a, b) in enumerate(
            [(seg_hbm, seg), (gain_hbm, gain), (wqkv_hbm, wqkv), (g_hbm, g), (wout_hbm, wout),
             (ma_hbm, ma), (mo_hbm, mo), (se_hbm, se)]
        )
    ]
    for one in local:
        one.start()

    barrier = pltpu.get_barrier_semaphore()
    for dev in (prv, along_y(1), along_y(2), along_y(3), along_z(-1)):
        pl.semaphore_signal(barrier, inc=1, device_id=dev, device_id_type=MESH)

    @pl.when((c >= 2) & (c < 7))
    def _():
        pl.semaphore_signal(barrier, inc=1, device_id=up, device_id_type=MESH)

    pl.semaphore_wait(barrier, 5 + (c >= 3).astype(jnp.int32))
    pl.semaphore_signal(said.at[0], inc=1, device_id=up, device_id_type=MESH)

    def known(i):
        pl.semaphore_wait(said.at[i], 1 if i == 0 else 2)
        if i < 6:
            far_by = 1 if i < 3 else 4
            for by in (far_by, -far_by):
                pl.semaphore_signal(said.at[i + 1], inc=1, device_id=along_z(by), device_id_type=MESH)

    def x_copy(r):
        rows = pl.ds(r * HALF, HALF)
        return remote(x_hbm.at[rows], xin.at[rows], xs.at[r], xr.at[r], nxt)

    def group(j):
        return lax.rem(z + 3 - j, 4)

    def y_copy(u, j, i):
        src = gb.at[u, group(j), :, lax.rem(y + i, 4)]
        return remote(src, yin.at[u, j, i - 1], ys.at[u, j, i - 1], yr.at[u, j, i - 1], along_y(i))

    for r in range(2):
        x_copy(r).start()
    local[3].wait()
    for u in range(2):
        for j in range(4):
            gb[u, group(j)] = g[u, group(j)].astype(BF16)
            for i in (1, 2, 3):
                y_copy(u, j, i).start()

    def kv_copy(k, r):
        return remote(kv.at[k, r], kv.at[k + 1, r], ks.at[k, r], kr.at[k, r], up)

    def project(r):
        rows = pl.ds(r * HALF, HALF)
        x_copy(r).wait_recv()
        values = xin[rows, :].astype(F32)
        meansq = jnp.mean(values * values, axis=-1, keepdims=True)
        normed = (values * lax.rsqrt(meansq + eps_norm) * gain[...]).astype(BF16)
        nrm[rows, :] = normed
        both = jnp.dot(normed, wqkv[:, HC:], preferred_element_type=F32).astype(BF16)
        for t in range(2):
            for h in range(H):
                kv[0, r, t, h] = both[:, t * HC + h * DH : t * HC + (h + 1) * DH]

        @pl.when(c < 7)
        def _():
            kv_copy(0, r).start()

    def q_copy(i):
        return remote(qs.at[i], qs.at[i + 1], qss.at[i], qrs.at[i], down)


    def attend(i, k, r):
        mask = segk[k, r] == segq[i]
        if k == 0:
            place = lax.broadcasted_iota(jnp.int32, (HALF, ROWS), 0) + r * HALF
            mask = mask & (place <= lax.broadcasted_iota(jnp.int32, (HALF, ROWS), 1))
        first = (i > 0 or k == 0) and r == 0
        for h in range(H):
            s = lax.dot_general(
                kv[k, r, 0, h], qs[i, h], (((1,), (1,)), ((), ())), preferred_element_type=F32
            )
            s = jnp.where(mask, s * (DH ** (-0.5)), NEG)
            top = jnp.max(s, axis=0, keepdims=True)
            if not first:
                old = ms[i, h]
                top = jnp.maximum(old, top)
            w = jnp.exp(s - top)
            total = jnp.sum(w, axis=0, keepdims=True)
            value = lax.dot_general(
                kv[k, r, 1, h], w.astype(BF16), (((0,), (0,)), ((), ())), preferred_element_type=F32
            )
            if not first:
                shrink = jnp.exp(old - top)
                total = total + shrink * ls[i, h]
                value = value + shrink * acc[i, h]
            ms[i, h] = top
            ls[i, h] = total
            acc[i, h] = value

    def kv_arrived(k, r):
        @pl.when(c >= k)
        def _():
            kv_copy(k - 1, r).wait_recv()

        if k == 1:
            @pl.when((c >= 1) & (c < 7))
            def _():
                kv_copy(1, r).start()

        @pl.when(c >= k)
        def _():
            attend(0, k, r)

    def part_copy(n, u):
        return (
            remote(part.at[n, u], part.at[n + 1, u], ps.at[n // 2, u, 0], pr.at[n // 2, u, 0], up),
            remote(stat.at[n, u], stat.at[n + 1, u], ps.at[n // 2, u, 1], pr.at[n // 2, u, 1], up),
        )

    def merged(i, n, h):
        u, v = divmod(h, 2)
        m, t = stat[n, u, 2 * v : 2 * v + 1, :], stat[n, u, 2 * v + 1 : 2 * v + 2, :]
        top = jnp.maximum(ms[i, h], m)
        mine, other = jnp.exp(ms[i, h] - top), t * jnp.exp(m - top)
        ms[i, h] = top
        ls[i, h] = mine * ls[i, h] + other
        acc[i, h] = mine * acc[i, h] + other * part[n, u, v].astype(F32)

    def send_part(i, n, u):
        for v in range(2):
            h = 2 * u + v
            part[n, u, v] = (acc[i, h] / ls[i, h]).astype(BF16)
            stat[n, u, 2 * v : 2 * v + 1, :] = ms[i, h]
            stat[n, u, 2 * v + 1 : 2 * v + 2, :] = ls[i, h]
        for one in part_copy(n, u):
            one.start()

    def take_part(i, n, u):
        for one in part_copy(n - 1, u):
            one.wait_recv()
        for v in range(2):
            merged(i, n, 2 * u + v)

    def w_copy(u, j):
        return remote(sent.at[u, j], win.at[u, j], ws.at[u, j], wr.at[u, j], along_z(-1 - j))

    def y_sum(u, j):
        for i in (1, 2, 3):
            y_copy(u, j, i).wait_recv()
        total = g[u, group(j), :, y]
        for i in range(3):
            total = total + yin[u, j, i].astype(F32)
        if j == 3:
            red[u] = total
        else:
            sent[u, j] = total.astype(BF16)
        if j < 3:
            w_copy(u, j).start()

    def f_copy(i):
        at = lax.rem(z + 32 - 4 * i, 32)
        src = sent.at[lax.div(lax.rem(at, 8), 4), 3, lax.div(at, 8)]
        return remote(src, far.at[i - 1], fs.at[i - 1], fr.at[i - 1], along_z(-4 * i))

    def w_sum(u):
        for j in range(3):
            w_copy(u, j).wait_recv()
        total = red[u]
        for j in range(3):
            total = total + win[u, j].astype(F32)
        red[u] = total
        sent[u, 3] = total.astype(BF16)

        @pl.when(lax.div(c, 4) == u)
        def _():
            for i in (4, 2, 6):
                f_copy(i).start()

        @pl.when(lax.div(c, 4) != u)
        def _():
            for i in (3, 5, 1, 7):
                f_copy(i).start()

    for i in (0, 1, 2):
        local[i].wait()
    project(0)
    project(1)
    queries = jnp.dot(nrm[...], wqkv[:, :HC], preferred_element_type=F32).astype(BF16)
    for h in range(H):
        qs[0, h] = queries[:, h * DH : (h + 1) * DH]

    @pl.when(c >= 3)
    def _():
        q_copy(0).start()

    for k in range(3):
        for r in range(2):
            at = jnp.maximum(2 * (c - k) + r, 0)
            cols = jnp.transpose(jnp.broadcast_to(seg[pl.ds(at, 1), :], (HALF, HALF)))
            segk[k, r] = jnp.concatenate([cols, cols], axis=1)
    for i in range(3):
        at = 2 * jnp.minimum(c + i, 7)
        segq[i] = jnp.concatenate([seg[pl.ds(at, 1), :], seg[pl.ds(at + 1, 1), :]], axis=1)
    attend(0, 0, 0)
    attend(0, 0, 1)
    known(0)
    y_sum(0, 0)
    known(1)
    y_sum(0, 1)
    known(2)
    y_sum(0, 2)
    kv_arrived(1, 0)
    y_sum(0, 3)
    known(3)

    @pl.when((c >= 2) & (c < 7))
    def _():
        q_copy(0).wait_recv()

    @pl.when((c >= 3) & (c < 7))
    def _():
        q_copy(1).start()

    y_sum(1, 0)
    kv_arrived(1, 1)
    known(4)
    y_sum(1, 1)
    known(5)
    y_sum(1, 2)
    known(6)
    w_sum(0)
    y_sum(1, 3)
    kv_arrived(2, 0)

    @pl.when((c >= 2) & (c < 7))
    def _():
        attend(1, 2, 0)

    @pl.when((c >= 2) & (c < 6))
    def _():
        q_copy(1).wait_recv()
        attend(2, 2, 0)

    w_sum(1)

    @pl.when(c >= 2)
    def _():
        kv_copy(1, 1).wait_recv()

    @pl.when((c >= 2) & (c < 6))
    def _():
        attend(2, 2, 1)
        send_part(2, 0, 0)
        send_part(2, 0, 1)

    @pl.when((c >= 2) & (c < 7))
    def _():
        attend(1, 2, 1)

    for u in range(2):
        @pl.when((c >= 3) & (c < 7))
        def _():
            take_part(1, 1, u)

        @pl.when((c >= 2) & (c < 7))
        def _():
            send_part(1, 2, u)

        if u == 0:
            @pl.when(c >= 2)
            def _():
                attend(0, 2, 1)

    local[4].wait()
    for u in range(2):
        @pl.when(c >= 3)
        def _():
            take_part(0, 3, u)

    attended = jnp.concatenate([(acc[0, h] / ls[0, h]).astype(BF16) for h in range(H)], axis=0)
    final = lax.dot_general(attended, wout[...], (((0,), (0,)), ((), ())), preferred_element_type=F32)
    ov[...] = (final + xin[...].astype(F32)).astype(BF16)

    for i in (5, 6, 7):
        local[i].wait()
    for i in range(1, 8):
        f_copy(i).wait_recv()
    grad = red[lax.div(c, 4), zh]
    for i in range(7):
        grad = grad + far[i].astype(F32)
    new_moment = beta_one * mo[...] + (1.0 - beta_one) * grad
    new_second = beta_two * se[...] + (1.0 - beta_two) * grad * grad
    update = new_moment / fix_one / (jnp.sqrt(new_second / fix_two) + adam_eps) + decay * ma[...]
    nma[...] = ma[...] - rate * update
    nmo[...] = new_moment
    nse[...] = new_second
    for r in range(2):
        x_copy(r).wait_send()
    for u in range(2):
        for j in range(4):
            for i in (1, 2, 3):
                y_copy(u, j, i).wait_send()
        for j in range(3):
            w_copy(u, j).wait_send()
    for i in range(1, 8):
        f_copy(i).wait_send()
    for k in range(2):
        @pl.when((c >= k) & (c < 7))
        def _():
            for r in range(2):
                kv_copy(k, r).wait_send()

    @pl.when(c >= 3)
    def _():
        q_copy(0).wait_send()

    @pl.when((c >= 3) & (c < 7))
    def _():
        q_copy(1).wait_send()

    for n, last in ((0, 6), (2, 7)):
        @pl.when((c >= 2) & (c < last))
        def _():
            for u in range(2):
                for one in part_copy(n, u):
                    one.wait_send()


def hand_over(*refs):
    sems = refs[8]
    copies = [pltpu.make_async_copy(refs[i], refs[4 + i], sems.at[i]) for i in range(4)]
    for one in copies:
        one.start()
    for one in copies:
        one.wait()


def on_device(section_held, segments, norm_gain, w_qkv, w_out, grad_parts, master, moment, second):
    shard_rows = (32, 128)
    any_spec = pl.BlockSpec(memory_space=pl.ANY)
    vmem_spec = pl.BlockSpec(memory_space=pltpu.VMEM)
    vmem, dma = pltpu.VMEM, pltpu.SemaphoreType.DMA
    outs = pl.pallas_call(
        kernel,
        out_shape=(
            vmem((ROWS, D), BF16),
            vmem(shard_rows, F32),
            vmem(shard_rows, F32),
            vmem(shard_rows, F32),
        ),
        in_specs=[pl.BlockSpec(memory_space=pltpu.HBM)] * 9,
        out_specs=[vmem_spec] * 4,
        scratch_shapes=[
            vmem((ROWS, D), BF16),
            vmem((ROWS, D), BF16),
            vmem((D, 3 * HC), BF16),
            vmem((HC, D), BF16),
            vmem((1, D), F32),
            vmem((16, 128), jnp.int32),
            vmem((3, 2, HALF, ROWS), jnp.int32),
            vmem((3, 1, ROWS), jnp.int32),
            vmem((3, 2, 2, H, HALF, DH), BF16),
            vmem((3, H, ROWS, DH), BF16),
            vmem((3, H, DH, ROWS), F32),
            vmem((3, H, 1, ROWS), F32),
            vmem((3, H, 1, ROWS), F32),
            vmem((4, 2, 2, DH, ROWS), BF16),
            vmem((4, 2, 4, ROWS), F32),
            vmem((2, 4, 4, 4, 32, 128), F32),
            vmem((2, 4, 4, 4, 32, 128), BF16),
            vmem((2, 4, 3, 4, 32, 128), BF16),
            vmem((2, 4, 32, 128), F32),
            vmem((2, 4, 4, 32, 128), BF16),
            vmem((2, 3, 4, 32, 128), BF16),
            vmem((7, 32, 128), BF16),
            vmem(shard_rows, F32),
            vmem(shard_rows, F32),
            vmem(shard_rows, F32),
            dma((8,)),
            dma((2,)), dma((2,)),
            dma((2, 4, 3)), dma((2, 4, 3)),
            dma((2, 2)), dma((2, 2)),
            dma((2,)), dma((2,)),
            dma((2, 2, 2)), dma((2, 2, 2)),
            dma((2, 3)), dma((2, 3)),
            dma((7,)), dma((7,)),
            pltpu.SemaphoreType.REGULAR((7,)),
        ],
        compiler_params=pltpu.CompilerParams(
            collective_id=0, has_side_effects=True, vmem_limit_bytes=48 << 20
        ),
    )(
        *(pltpu.with_memory_space_constraint(one, pltpu.HBM) for one in (
            section_held.reshape(ROWS, D),
            segments.reshape(16, 128),
            norm_gain,
            w_qkv[0],
            w_out[0],
            grad_parts.reshape(2, 4, 4, 4, 32, 128),
            master.reshape(shard_rows),
            moment.reshape(shard_rows),
            second.reshape(shard_rows),
        ))
    )
    outs = pl.pallas_call(
        hand_over,
        out_shape=[jax.ShapeDtypeStruct(one.shape, one.dtype) for one in outs],
        in_specs=[any_spec] * 4,
        out_specs=[any_spec] * 4,
        scratch_shapes=[dma((4,))],
        compiler_params=pltpu.CompilerParams(vmem_limit_bytes=4 << 20),
    )(*outs)
    return (
        outs[0].reshape(section_held.shape),
        outs[1].reshape(master.shape),
        outs[2].reshape(moment.shape),
        outs[3].reshape(second.shape),
    )


def solution(mesh):
    in_specs = (
        P("pipe", "dp", "ctx", None),
        P("pipe", "dp", None),
        P("pipe", None),
        P("pipe", None, None),
        P("pipe", None, None),
        P("pipe", "ctx", "dp", None),
        P("pipe", ("ctx", "dp")),
        P("pipe", ("ctx", "dp")),
        P("pipe", ("ctx", "dp")),
    )
    out_specs = (
        P("pipe", "dp", "ctx", None),
        P("pipe", ("ctx", "dp")),
        P("pipe", ("ctx", "dp")),
        P("pipe", ("ctx", "dp")),
    )
    return jax.shard_map(
        on_device, mesh=mesh, in_specs=in_specs, out_specs=out_specs, check_vma=False
    )
```

```python
import functools

import jax
import jax.numpy as jnp
from jax import lax
from jax.experimental import pallas as pl
from jax.experimental.pallas import tpu as pltpu
from jax.sharding import PartitionSpec as P

H = 4
DH = 128
D = 1024
ROWS = 256
HALF = 128
HC = H * DH
NEG = -1e30

eps_norm = 1e-06
rate = 0.001
beta_one = 0.9
beta_two = 0.999
adam_eps = 1e-08
decay = 0.1
fix_one = 0.9999734386011124
fix_two = 0.09520785288629038

MESH = pl.DeviceIdType.MESH
F32 = jnp.float32
BF16 = jnp.bfloat16


def kernel(
    x_hbm, seg_hbm, gain_hbm, wqkv_hbm, wout_hbm, g_hbm, ma_hbm, mo_hbm, se_hbm,
    ov, nma, nmo, nse,
    xin, nrm, wqkv, wout, gain, seg, segk, segq, kv, qs, acc, ms, ls, part, stat,
    g, gb, yin, red, sent, win, far, ma, mo, se,
    loc, xs, xr, ys, yr, ks, kr, qss, qrs, ps, pr, ws, wr, fs, fr, said,
):
    p, c, d = lax.axis_index("pipe"), lax.axis_index("ctx"), lax.axis_index("dp")
    zh, y = lax.div(d, 4), lax.rem(d, 4)
    z = zh * 8 + c
    nxt, prv = (lax.rem(p + 1, 8), c, d), (lax.rem(p + 7, 8), c, d)

    def along_y(by):
        return p, c, zh * 4 + lax.rem(y + by, 4)

    def along_z(by):
        at = lax.rem(z + by + 32, 32)
        return p, lax.rem(at, 8), lax.div(at, 8) * 4 + y

    up, down = along_z(1), along_z(-1)

    def remote(src, dst, ssem, rsem, dev):
        return pltpu.make_async_remote_copy(
            src_ref=src, dst_ref=dst, send_sem=ssem, recv_sem=rsem, device_id=dev, device_id_type=MESH
        )

    local = [
        pltpu.make_async_copy(a, b, loc.at[i])
        for i, (a, b) in enumerate(
            [(seg_hbm, seg), (gain_hbm, gain), (wqkv_hbm, wqkv), (g_hbm, g), (wout_hbm, wout),
             (ma_hbm, ma), (mo_hbm, mo), (se_hbm, se)]
        )
    ]
    for one in local:
        one.start()

    barrier = pltpu.get_barrier_semaphore()
    for dev in (prv, along_y(1), along_y(2), along_y(3), along_z(-1)):
        pl.semaphore_signal(barrier, inc=1, device_id=dev, device_id_type=MESH)

    @pl.when((c >= 2) & (c < 7))
    def _():
        pl.semaphore_signal(barrier, inc=1, device_id=up, device_id_type=MESH)

    pl.semaphore_wait(barrier, 5 + (c >= 3).astype(jnp.int32))
    pl.semaphore_signal(said.at[0], inc=1, device_id=up, device_id_type=MESH)

    def known(i):
        pl.semaphore_wait(said.at[i], 1 if i == 0 else 2)
        if i < 6:
            far_by = 1 if i < 3 else 4
            for by in (far_by, -far_by):
                pl.semaphore_signal(said.at[i + 1], inc=1, device_id=along_z(by), device_id_type=MESH)

    def x_copy(r):
        rows = pl.ds(r * HALF, HALF)
        return remote(x_hbm.at[rows], xin.at[rows], xs.at[r], xr.at[r], nxt)

    def group(j):
        return lax.rem(z + 3 - j, 4)

    def y_copy(u, j, i):
        src = gb.at[u, group(j), :, lax.rem(y + i, 4)]
        return remote(src, yin.at[u, j, i - 1], ys.at[u, j, i - 1], yr.at[u, j, i - 1], along_y(i))

    for r in range(2):
        x_copy(r).start()
    local[3].wait()
    for u in range(2):
        for j in range(4):
            gb[u, group(j)] = g[u, group(j)].astype(BF16)
            for i in (1, 2, 3):
                y_copy(u, j, i).start()

    def kv_copy(k, r):
        return remote(kv.at[k, r], kv.at[k + 1, r], ks.at[k, r], kr.at[k, r], up)

    def project(r):
        rows = pl.ds(r * HALF, HALF)
        x_copy(r).wait_recv()
        values = xin[rows, :].astype(F32)
        meansq = jnp.mean(values * values, axis=-1, keepdims=True)
        normed = (values * lax.rsqrt(meansq + eps_norm) * gain[...]).astype(BF16)
        nrm[rows, :] = normed
        both = jnp.dot(normed, wqkv[:, HC:], preferred_element_type=F32).astype(BF16)
        for t in range(2):
            for h in range(H):
                kv[0, r, t, h] = both[:, t * HC + h * DH : t * HC + (h + 1) * DH]

        @pl.when(c < 7)
        def _():
            kv_copy(0, r).start()

    def q_copy(i):
        return remote(qs.at[i], qs.at[i + 1], qss.at[i], qrs.at[i], down)


    def attend(i, k, r):
        mask = segk[k, r] == segq[i]
        if k == 0:
            place = lax.broadcasted_iota(jnp.int32, (HALF, ROWS), 0) + r * HALF
            mask = mask & (place <= lax.broadcasted_iota(jnp.int32, (HALF, ROWS), 1))
        first = (i > 0 or k == 0) and r == 0
        for h in range(H):
            s = lax.dot_general(
                kv[k, r, 0, h], qs[i, h], (((1,), (1,)), ((), ())), preferred_element_type=F32
            )
            s = jnp.where(mask, s * (DH ** (-0.5)), NEG)
            top = jnp.max(s, axis=0, keepdims=True)
            if not first:
                old = ms[i, h]
                top = jnp.maximum(old, top)
            w = jnp.exp(s - top)
            total = jnp.sum(w, axis=0, keepdims=True)
            value = lax.dot_general(
                kv[k, r, 1, h], w.astype(BF16), (((0,), (0,)), ((), ())), preferred_element_type=F32
            )
            if not first:
                shrink = jnp.exp(old - top)
                total = total + shrink * ls[i, h]
                value = value + shrink * acc[i, h]
            ms[i, h] = top
            ls[i, h] = total
            acc[i, h] = value

    def kv_arrived(k, r):
        @pl.when(c >= k)
        def _():
            kv_copy(k - 1, r).wait_recv()

        if k == 1:
            @pl.when((c >= 1) & (c < 7))
            def _():
                kv_copy(1, r).start()

        @pl.when(c >= k)
        def _():
            attend(0, k, r)

    def part_copy(n, u):
        return (
            remote(part.at[n, u], part.at[n + 1, u], ps.at[n // 2, u, 0], pr.at[n // 2, u, 0], up),
            remote(stat.at[n, u], stat.at[n + 1, u], ps.at[n // 2, u, 1], pr.at[n // 2, u, 1], up),
        )

    def merged(i, n, h):
        u, v = divmod(h, 2)
        m, t = stat[n, u, 2 * v : 2 * v + 1, :], stat[n, u, 2 * v + 1 : 2 * v + 2, :]
        top = jnp.maximum(ms[i, h], m)
        mine, other = jnp.exp(ms[i, h] - top), t * jnp.exp(m - top)
        ms[i, h] = top
        ls[i, h] = mine * ls[i, h] + other
        acc[i, h] = mine * acc[i, h] + other * part[n, u, v].astype(F32)

    def send_part(i, n, u):
        for v in range(2):
            h = 2 * u + v
            part[n, u, v] = (acc[i, h] / ls[i, h]).astype(BF16)
            stat[n, u, 2 * v : 2 * v + 1, :] = ms[i, h]
            stat[n, u, 2 * v + 1 : 2 * v + 2, :] = ls[i, h]
        for one in part_copy(n, u):
            one.start()

    def take_part(i, n, u):
        for one in part_copy(n - 1, u):
            one.wait_recv()
        for v in range(2):
            merged(i, n, 2 * u + v)

    def w_copy(u, j):
        return remote(sent.at[u, j], win.at[u, j], ws.at[u, j], wr.at[u, j], along_z(-1 - j))

    def y_sum(u, j):
        for i in (1, 2, 3):
            y_copy(u, j, i).wait_recv()
        total = g[u, group(j), :, y]
        for i in range(3):
            total = total + yin[u, j, i].astype(F32)
        if j == 3:
            red[u] = total
        else:
            sent[u, j] = total.astype(BF16)
        if j < 3:
            w_copy(u, j).start()

    def f_copy(i):
        at = lax.rem(z + 32 - 4 * i, 32)
        src = sent.at[lax.div(lax.rem(at, 8), 4), 3, lax.div(at, 8)]
        return remote(src, far.at[i - 1], fs.at[i - 1], fr.at[i - 1], along_z(-4 * i))

    def w_sum(u):
        for j in range(3):
            w_copy(u, j).wait_recv()
        total = red[u]
        for j in range(3):
            total = total + win[u, j].astype(F32)
        red[u] = total
        sent[u, 3] = total.astype(BF16)

        @pl.when(lax.div(c, 4) == u)
        def _():
            for i in (4, 2, 6):
                f_copy(i).start()

        @pl.when(lax.div(c, 4) != u)
        def _():
            for i in (3, 5, 1, 7):
                f_copy(i).start()

    for i in (0, 1, 2):
        local[i].wait()
    project(0)
    project(1)
    queries = jnp.dot(nrm[...], wqkv[:, :HC], preferred_element_type=F32).astype(BF16)
    for h in range(H):
        qs[0, h] = queries[:, h * DH : (h + 1) * DH]

    @pl.when(c >= 3)
    def _():
        q_copy(0).start()

    for k in range(3):
        for r in range(2):
            at = jnp.maximum(2 * (c - k) + r, 0)
            cols = jnp.transpose(jnp.broadcast_to(seg[pl.ds(at, 1), :], (HALF, HALF)))
            segk[k, r] = jnp.concatenate([cols, cols], axis=1)
    for i in range(3):
        at = 2 * jnp.minimum(c + i, 7)
        segq[i] = jnp.concatenate([seg[pl.ds(at, 1), :], seg[pl.ds(at + 1, 1), :]], axis=1)
    known(0)
    y_sum(0, 0)
    known(1)
    y_sum(0, 1)
    known(2)
    y_sum(0, 2)
    y_sum(0, 3)
    attend(0, 0, 0)
    attend(0, 0, 1)
    known(3)
    y_sum(1, 0)
    kv_arrived(1, 0)
    known(4)
    y_sum(1, 1)
    y_sum(1, 2)

    @pl.when((c >= 2) & (c < 7))
    def _():
        q_copy(0).wait_recv()

    @pl.when((c >= 3) & (c < 7))
    def _():
        q_copy(1).start()

    known(5)
    y_sum(1, 3)
    kv_arrived(1, 1)
    kv_arrived(2, 0)

    @pl.when((c >= 2) & (c < 7))
    def _():
        attend(1, 2, 0)

    @pl.when((c >= 2) & (c < 6))
    def _():
        q_copy(1).wait_recv()
        attend(2, 2, 0)

    known(6)
    w_sum(0)
    w_sum(1)
    @pl.when(c >= 2)
    def _():
        kv_copy(1, 1).wait_recv()

    @pl.when((c >= 2) & (c < 6))
    def _():
        attend(2, 2, 1)
        send_part(2, 0, 0)
        send_part(2, 0, 1)

    @pl.when((c >= 2) & (c < 7))
    def _():
        attend(1, 2, 1)

    for u in range(2):
        @pl.when((c >= 3) & (c < 7))
        def _():
            take_part(1, 1, u)

        @pl.when((c >= 2) & (c < 7))
        def _():
            send_part(1, 2, u)

        if u == 0:
            @pl.when(c >= 2)
            def _():
                attend(0, 2, 1)

    local[4].wait()
    for u in range(2):
        @pl.when(c >= 3)
        def _():
            take_part(0, 3, u)

    attended = jnp.concatenate([(acc[0, h] / ls[0, h]).astype(BF16) for h in range(H)], axis=0)
    final = lax.dot_general(attended, wout[...], (((0,), (0,)), ((), ())), preferred_element_type=F32)
    ov[...] = (final + xin[...].astype(F32)).astype(BF16)

    for i in (5, 6, 7):
        local[i].wait()
    for i in range(1, 8):
        f_copy(i).wait_recv()
    grad = red[lax.div(c, 4), zh]
    for i in range(7):
        grad = grad + far[i].astype(F32)
    new_moment = beta_one * mo[...] + (1.0 - beta_one) * grad
    new_second = beta_two * se[...] + (1.0 - beta_two) * grad * grad
    update = new_moment / fix_one / (jnp.sqrt(new_second / fix_two) + adam_eps) + decay * ma[...]
    nma[...] = ma[...] - rate * update
    nmo[...] = new_moment
    nse[...] = new_second
    for r in range(2):
        x_copy(r).wait_send()
    for u in range(2):
        for j in range(4):
            for i in (1, 2, 3):
                y_copy(u, j, i).wait_send()
        for j in range(3):
            w_copy(u, j).wait_send()
    for i in range(1, 8):
        f_copy(i).wait_send()
    for k in range(2):
        @pl.when((c >= k) & (c < 7))
        def _():
            for r in range(2):
                kv_copy(k, r).wait_send()

    @pl.when(c >= 3)
    def _():
        q_copy(0).wait_send()

    @pl.when((c >= 3) & (c < 7))
    def _():
        q_copy(1).wait_send()

    for n, last in ((0, 6), (2, 7)):
        @pl.when((c >= 2) & (c < last))
        def _():
            for u in range(2):
                for one in part_copy(n, u):
                    one.wait_send()


def hand_over(*refs):
    sems = refs[8]
    copies = [pltpu.make_async_copy(refs[i], refs[4 + i], sems.at[i]) for i in range(4)]
    for one in copies:
        one.start()
    for one in copies:
        one.wait()


def on_device(section_held, segments, norm_gain, w_qkv, w_out, grad_parts, master, moment, second):
    shard_rows = (32, 128)
    any_spec = pl.BlockSpec(memory_space=pl.ANY)
    vmem_spec = pl.BlockSpec(memory_space=pltpu.VMEM)
    vmem, dma = pltpu.VMEM, pltpu.SemaphoreType.DMA
    outs = pl.pallas_call(
        kernel,
        out_shape=(
            vmem((ROWS, D), BF16),
            vmem(shard_rows, F32),
            vmem(shard_rows, F32),
            vmem(shard_rows, F32),
        ),
        in_specs=[pl.BlockSpec(memory_space=pltpu.HBM)] * 9,
        out_specs=[vmem_spec] * 4,
        scratch_shapes=[
            vmem((ROWS, D), BF16),
            vmem((ROWS, D), BF16),
            vmem((D, 3 * HC), BF16),
            vmem((HC, D), BF16),
            vmem((1, D), F32),
            vmem((16, 128), jnp.int32),
            vmem((3, 2, HALF, ROWS), jnp.int32),
            vmem((3, 1, ROWS), jnp.int32),
            vmem((3, 2, 2, H, HALF, DH), BF16),
            vmem((3, H, ROWS, DH), BF16),
            vmem((3, H, DH, ROWS), F32),
            vmem((3, H, 1, ROWS), F32),
            vmem((3, H, 1, ROWS), F32),
            vmem((4, 2, 2, DH, ROWS), BF16),
            vmem((4, 2, 4, ROWS), F32),
            vmem((2, 4, 4, 4, 32, 128), F32),
            vmem((2, 4, 4, 4, 32, 128), BF16),
            vmem((2, 4, 3, 4, 32, 128), BF16),
            vmem((2, 4, 32, 128), F32),
            vmem((2, 4, 4, 32, 128), BF16),
            vmem((2, 3, 4, 32, 128), BF16),
            vmem((7, 32, 128), BF16),
            vmem(shard_rows, F32),
            vmem(shard_rows, F32),
            vmem(shard_rows, F32),
            dma((8,)),
            dma((2,)), dma((2,)),
            dma((2, 4, 3)), dma((2, 4, 3)),
            dma((2, 2)), dma((2, 2)),
            dma((2,)), dma((2,)),
            dma((2, 2, 2)), dma((2, 2, 2)),
            dma((2, 3)), dma((2, 3)),
            dma((7,)), dma((7,)),
            pltpu.SemaphoreType.REGULAR((7,)),
        ],
        compiler_params=pltpu.CompilerParams(
            collective_id=0, has_side_effects=True, vmem_limit_bytes=48 << 20
        ),
    )(
        *(pltpu.with_memory_space_constraint(one, pltpu.HBM) for one in (
            section_held.reshape(ROWS, D),
            segments.reshape(16, 128),
            norm_gain,
            w_qkv[0],
            w_out[0],
            grad_parts.reshape(2, 4, 4, 4, 32, 128),
            master.reshape(shard_rows),
            moment.reshape(shard_rows),
            second.reshape(shard_rows),
        ))
    )
    outs = pl.pallas_call(
        hand_over,
        out_shape=[jax.ShapeDtypeStruct(one.shape, one.dtype) for one in outs],
        in_specs=[any_spec] * 4,
        out_specs=[any_spec] * 4,
        scratch_shapes=[dma((4,))],
        compiler_params=pltpu.CompilerParams(vmem_limit_bytes=4 << 20),
    )(*outs)
    return (
        outs[0].reshape(section_held.shape),
        outs[1].reshape(master.shape),
        outs[2].reshape(moment.shape),
        outs[3].reshape(second.shape),
    )


def solution(mesh):
    in_specs = (
        P("pipe", "dp", "ctx", None),
        P("pipe", "dp", None),
        P("pipe", None),
        P("pipe", None, None),
        P("pipe", None, None),
        P("pipe", "ctx", "dp", None),
        P("pipe", ("ctx", "dp")),
        P("pipe", ("ctx", "dp")),
        P("pipe", ("ctx", "dp")),
    )
    out_specs = (
        P("pipe", "dp", "ctx", None),
        P("pipe", ("ctx", "dp")),
        P("pipe", ("ctx", "dp")),
        P("pipe", ("ctx", "dp")),
    )
    return jax.shard_map(
        on_device, mesh=mesh, in_specs=in_specs, out_specs=out_specs, check_vma=False
    )
```
